32 devices in a mesh: dp: 16 (over z, x, core), mp: 2 (over y).
Axes of the slice: x: 2, y: 2, z: 4, core: 2. Of those that a mesh axis runs over, the one named last changes fastest.
Arguments:
- residual: bfloat16 [4096, 16, 768], P('mp', 'dp'), may hold values from -6 to 6
- out_grad: bfloat16 [4096, 16, 768], P('mp', 'dp'), may hold values from -6 to 6
- doc_bounds: int32 [16, 7], P('dp'), may hold values from 0 to 4096, as said below
- norm_gain: float32 [768], replicated, may hold values from 0.5 to 1.5
- proj_gate: bfloat16 [768, 1536], P(None, 'mp'), may hold values from -0.21875 to 0.21875
- proj_value: bfloat16 [768, 1536], P(None, 'mp'), may hold values from -0.21875 to 0.21875
- proj_state: bfloat16 [768, 256], replicated, may hold values from -0.21875 to 0.21875
- proj_step: bfloat16 [768, 48], P(None, 'mp'), may hold values from -0.21875 to 0.21875
- conv_value: float32 [4, 1536], P(None, 'mp'), may hold values from -3 to 3
- conv_value_bias: float32 [1536], P('mp'), may hold values from -3 to 3
- conv_state: float32 [4, 256], replicated, may hold values from -3 to 3
- conv_state_bias: float32 [256], replicated, may hold values from -3 to 3
- step_bias: float32 [48], P('mp'), may hold values from -6.9 to -2.3
- rate_log: float32 [24], P('mp'), may hold values from 0 to 2.77
- skip_gain: float32 [24], P('mp'), may hold values from 0.5 to 1.5
- skip_proj: bfloat16 [1536, 24], P('mp'), may hold values from -0.15625 to 0.15625
- mixer_gain: float32 [1536], P('mp'), may hold values from 0.5 to 1.5
- proj_out: bfloat16 [1536, 768], P('mp'), may hold values from -0.15625 to 0.15625
Outputs:
- output: bfloat16 [4096, 16, 768], P('mp', 'dp')
- grad_residual: float32 [4096, 16, 768], P('mp', 'dp')
- grad_norm_gain: float32 [768], replicated
- grad_proj_gate: float32 [768, 1536], P(None, 'mp')
- grad_proj_value: float32 [768, 1536], P(None, 'mp')
- grad_proj_state: float32 [768, 256], replicated
- grad_proj_step: float32 [768, 48], P(None, 'mp')
- grad_conv_value: float32 [4, 1536], P(None, 'mp')
- grad_conv_value_bias: float32 [1536], P('mp')
- grad_conv_state: float32 [4, 256], replicated
- grad_conv_state_bias: float32 [256], replicated
- grad_step_bias: float32 [48], P('mp')
- grad_rate_log: float32 [24], P('mp')
- grad_skip_gain: float32 [24], P('mp')
- grad_skip_proj: float32 [1536, 24], P('mp')
- grad_mixer_gain: float32 [1536], P('mp')
- grad_proj_out: float32 [1536, 768], P('mp')
The draws below stay inside these ranges and needn't reach their ends.
Inputs may be any that keep to these rules, and one draw needn't show every extreme that they name: `doc_bounds`: in each row the entries never fall: entry 0 is 0, entry k below 6 is where document k starts, and entry 6 is where the padding starts, at least 2049.
All inputs are finite; a program needn't handle non-finite values.
Results may differ from the reference program's by a relative error of at most 0.02.
Values may be sent and summed in bfloat16 or wider, within the bound.
No kernel may reach another device: no remote copies, remote signals or barrier semaphores. Data moves between devices by JAX's collectives and lax.ppermute only.
A program may use at most 640 MiB of HBM per device.

```python
import math
import jax
import jax.numpy as jnp
from jax import lax

D = 768
HEADS = 24
HEADDIM = 64
STATE = 64
CONV = 4
ROW_LEN = 4096
DOCS = 6
INNER = 1536
ROWS = 16
PAD_MAX = 2048


def draw_doc_bounds(key, part):
    key_base, key_power, key_pad, key_full = jax.random.split(jax.random.fold_in(key, 17), 4)
    base_len = jax.random.randint(key_base, (ROWS, DOCS), 8, 24)
    power_of = jax.random.randint(key_power, (ROWS, DOCS), 0, 6)
    weights_doc = jnp.left_shift(base_len, power_of)
    padding = jax.random.randint(key_pad, (ROWS,), 0, PAD_MAX)
    full_row = jax.random.randint(key_full, (), 0, ROWS)
    padding = jnp.where(jnp.arange(ROWS) == full_row, 0, padding)
    valid_len = ROW_LEN - padding
    running = jnp.cumsum(weights_doc, axis=1)
    ends_at = running * valid_len[:, None] // running[:, -1:]
    return jnp.concatenate([jnp.zeros((ROWS, 1), jnp.int32), ends_at.astype(jnp.int32)], 1)


def block_scale(rng, extent, cuts, smallest, top_value):
    loudness, own = 1.0, jax.random.fold_in(rng, 6)
    for dim, parts in cuts:
        draws = jnp.exp(jax.random.uniform(jax.random.fold_in(own, dim), (parts,), jnp.float32, smallest / len(cuts), top_value / len(cuts)))
        loudness = loudness * jnp.repeat(draws, extent[dim] // parts).reshape([-1 if axis == dim else 1 for axis in range(len(extent))])
    return loudness


def scatter_about(stream_key, dims, deviation, limit, pieces=(), kind=jnp.bfloat16):
    values = jax.random.normal(stream_key, dims, jnp.float32) * deviation
    if len(pieces) > 0:
        values = block_scale(stream_key, dims, pieces, -0.22, 0.18) * values
    return jnp.clip(values, min=-limit, max=limit).astype(kind)


def setup_inputs(seed: int = 0) -> dict:
    key_list = jax.random.split(jax.random.key(seed), 19)
    residual = scatter_about(key_list[0], (ROW_LEN, ROWS, D), 1.0, 6.0, ((0, 2), (1, 16)))
    out_grad = scatter_about(key_list[1], (ROW_LEN, ROWS, D), 1.0, 6.0, ((0, 2), (1, 16)))
    doc_bounds = draw_doc_bounds(jax.random.fold_in(key_list[18], 71), 0)
    norm_gain = jnp.clip(1.0 + 0.1 * jax.random.normal(key_list[3], (D,), jnp.float32), 0.5, 1.5)
    proj_gate = scatter_about(key_list[4], (D, INNER), D ** -0.5, 0.21875, ((1, 2),))
    proj_value = scatter_about(key_list[5], (D, INNER), D ** -0.5, 0.21875, ((1, 2),))
    proj_state = scatter_about(key_list[6], (D, 4 * STATE), D ** -0.5, 0.21875)
    proj_step = scatter_about(key_list[7], (D, 2 * HEADS), D ** -0.5, 0.21875, ((1, 2),))
    conv_value = scatter_about(key_list[8], (CONV, INNER), CONV ** -0.5, 3.0, ((1, 2),), jnp.float32)
    conv_value_bias = scatter_about(key_list[9], (INNER,), 0.5, 3.0, ((0, 2),), jnp.float32)
    conv_state = scatter_about(key_list[10], (CONV, 4 * STATE), CONV ** -0.5, 3.0, (), jnp.float32)
    conv_state_bias = scatter_about(key_list[11], (4 * STATE,), 0.5, 3.0, (), jnp.float32)
    step_bias = jnp.clip(-6.9 + 4.6000001430511475 * jax.random.uniform(key_list[12], (2 * HEADS,), jnp.float32) ** block_scale(key_list[12], (2 * HEADS,), ((0, 2),), -0.2, 0.2), -6.9, -2.3)
    rate_log = jnp.clip(2.77 * jax.random.uniform(key_list[13], (HEADS,), jnp.float32) ** block_scale(key_list[13], (HEADS,), ((0, 2),), -0.2, 0.2), 0.0, 2.77)
    skip_gain = jnp.clip(0.5 + 1.0 * jax.random.uniform(key_list[14], (HEADS,), jnp.float32) ** block_scale(key_list[14], (HEADS,), ((0, 2),), -0.2, 0.2), 0.5, 1.5)
    skip_proj = scatter_about(key_list[15], (INNER, HEADS), INNER ** -0.5, 0.15625, ((0, 2),))
    mixer_gain = jnp.clip(1.0 + 0.1 * jax.random.normal(key_list[16], (INNER,), jnp.float32), 0.5, 1.5)
    proj_out = scatter_about(key_list[17], (INNER, D), INNER ** -0.5, 0.15625, ((0, 2),))
    return dict(residual=residual, out_grad=out_grad, doc_bounds=doc_bounds, norm_gain=norm_gain, proj_gate=proj_gate, proj_value=proj_value, proj_state=proj_state, proj_step=proj_step, conv_value=conv_value, conv_value_bias=conv_value_bias, conv_state=conv_state, conv_state_bias=conv_state_bias, step_bias=step_bias, rate_log=rate_log, skip_gain=skip_gain, skip_proj=skip_proj, mixer_gain=mixer_gain, proj_out=proj_out)


epsilon = 1e-05
highest = lax.Precision.HIGHEST

@jax.custom_vjp
def low(v):
    return lax.optimization_barrier(v.astype(jnp.bfloat16)).astype(jnp.float32)

@jax.custom_vjp
def low_back(v):
    return v

def low_keep(v):
    return (low(v), None)

def low_pass(kept, grad):
    return (grad,)

def back_keep(v):
    return (v, None)

def back_low(kept, grad):
    return (low(grad),)
low.defvjp(low_keep, low_pass)
low_back.defvjp(back_keep, back_low)

def as_operand(values):
    return low_back(low(values))

def contract(form, left_op, right_op):
    return jnp.einsum(form, left_op, right_op, precision=highest)

def segment_sums(values):
    count_all = values.shape[-1]
    places = jnp.arange(count_all)
    repeated = jnp.broadcast_to(values[..., :, None], values.shape + (count_all,))
    lower_mask = places[:, None] > places[None, :]
    running = jnp.cumsum(jnp.where(lower_mask, repeated, 0.0), axis=-2)
    return jnp.where(places[:, None] >= places[None, :], running, -jnp.inf)

def scan_direction(inputs, step_size, decays, keys_in, read_out, segment):
    length, head_count, head_width = inputs.shape
    state_width = keys_in.shape[1]
    block_len = math.gcd(length, 128)
    blocks = length // block_len
    weighted = (inputs * step_size[:, :, None]).reshape(blocks, block_len, head_count, head_width)
    log_decay = jnp.transpose(decays.reshape(blocks, block_len, head_count), (0, 2, 1))
    key_block = keys_in.reshape(blocks, block_len, state_width)
    read_block = read_out.reshape(blocks, block_len, state_width)
    seg_block = segment.reshape(blocks, block_len)
    places = jnp.arange(block_len)
    strict = (places[:, None] > places[None, :])[None] & (seg_block[:, :, None] == seg_block[:, None, :])
    scores = contract('cin,cjn->cij', as_operand(read_block), as_operand(key_block))
    mixing = jnp.where(strict[:, None], jnp.exp(segment_sums(log_decay)), 0.0) * scores[:, None]
    inner_part = contract('chij,cjhp->cihp', as_operand(mixing), as_operand(weighted))
    running = jnp.cumsum(log_decay, axis=-1)
    to_end = jnp.exp(running[..., -1:] - running) * (seg_block == seg_block[:, -1:])[:, None, :]
    states = jnp.einsum('chj,cjn,cjhp->chpn', to_end, key_block, weighted, precision=highest)
    block_logs = jnp.transpose(running[..., -1])
    end_seg = seg_block[:, -1]
    carry_mix = jnp.exp(segment_sums(block_logs)) * (end_seg[:, None] == end_seg[None, :])[None]
    totals = jnp.einsum('hcd,dhpn->chpn', carry_mix, states, precision=highest)
    entering = jnp.concatenate([jnp.zeros_like(totals[:1]), totals[:-1]], 0)
    before = jnp.concatenate([seg_block[:1, :1], seg_block[:-1, -1:]], 0)
    reaching = jnp.exp(running) * (seg_block == before)[:, None, :]
    outer_part = jnp.einsum('cin,chpn,chi->cihp', read_block, entering, reaching, precision=highest)
    return (inner_part + outer_part).reshape(length, head_count, head_width)

def quasiseparable(mixed_in, gates_in, step_pre, step_bias, rate_log, segment):
    length, head_count, head_width = mixed_in.shape
    state_width = gates_in.shape[1] // 4
    step_size = jax.nn.softplus(step_pre.reshape(length, head_count, 2) + step_bias.reshape(head_count, 2))
    decays = -step_size * jnp.exp(rate_log)[:, None]
    forward_part = scan_direction(mixed_in, step_size[:, :, 0], decays[:, :, 0], gates_in[:, :state_width], gates_in[:, state_width:2 * state_width], segment)
    backward_part = scan_direction(mixed_in[::-1], step_size[::-1, :, 1], decays[::-1, :, 1], gates_in[::-1, 2 * state_width:3 * state_width], gates_in[::-1, 3 * state_width:], segment[::-1])
    return forward_part + backward_part[::-1]

def short_conv(signal, kernel, offset, segment):
    length = signal.shape[0]
    result = offset + kernel[0] * signal
    for shift_by in range(1, kernel.shape[0]):
        delayed = jnp.concatenate([jnp.zeros((shift_by, signal.shape[1]), signal.dtype), signal[:length - shift_by]], 0)
        delayed_seg = jnp.concatenate([jnp.full((shift_by,), -1, segment.dtype), segment[:length - shift_by]], 0)
        result = result + kernel[shift_by] * delayed * (delayed_seg == segment)[:, None]
    return result

def conv_silu(value_in, state_in, kernel_v, offset_v, kernel_s, offset_s, segment):
    return (jax.nn.silu(short_conv(value_in, kernel_v, offset_v, segment)), jax.nn.silu(short_conv(state_in, kernel_s, offset_s, segment)))

def segments_of(doc_bounds, length):
    places = jnp.arange(length, dtype=jnp.int32)
    segment = lax.optimization_barrier(jnp.sum((places[None, :, None] >= doc_bounds[:, None, :]).astype(jnp.int32), -1))
    valid_mask = (places[None, :] < doc_bounds[:, -1:]).astype(jnp.float32)
    return (segment, valid_mask)

def product(left_op, right_op):
    return jnp.dot(left_op, right_op, precision=highest, preferred_element_type=jnp.float32)

def branch_row(row_in, segment, valid_mask, params):
    norm_gain, proj_gate, proj_value, proj_state, proj_step, conv_value, conv_value_bias, conv_state, conv_state_bias, step_bias, rate_log, skip_gain, skip_proj, mixer_gain, proj_out = params
    scale_in = lax.rsqrt(lax.optimization_barrier(jnp.mean(row_in * row_in, -1, keepdims=True)) + epsilon)
    normed = low(row_in * scale_in * norm_gain)
    gate_pre = low_back(product(normed, proj_gate))
    value_pre = low_back(product(normed, proj_value))
    step_pre = low_back(product(normed, proj_step))
    state_pre = product(normed, proj_state)
    value_act, state_act = conv_silu(value_pre, state_pre, conv_value, conv_value_bias, conv_state, conv_state_bias, segment)
    value_act = low(value_act)
    state_act = low(state_act)
    length = row_in.shape[0]
    heads_view = value_act.reshape(length, HEADS, HEADDIM)
    scanned = quasiseparable(heads_view, state_act, step_pre, step_bias, rate_log, segment)
    skip_coef = product(value_act, skip_proj) + skip_gain
    mixed = (scanned + skip_coef[:, :, None] * heads_view).reshape(length, HEADS * HEADDIM)
    gated = mixed * jax.nn.silu(gate_pre) * valid_mask[:, None]
    normed_out = low(gated * lax.rsqrt(lax.optimization_barrier(jnp.mean(gated * gated, -1, keepdims=True)) + epsilon) * mixer_gain)
    return product(normed_out, proj_out)

def reference(residual, out_grad, doc_bounds, norm_gain, proj_gate, proj_value, proj_state, proj_step, conv_value, conv_value_bias, conv_state, conv_state_bias, step_bias, rate_log, skip_gain, skip_proj, mixer_gain, proj_out):
    params = tuple((weight_in.astype(jnp.float32) for weight_in in (norm_gain, proj_gate, proj_value, proj_state, proj_step, conv_value, conv_value_bias, conv_state, conv_state_bias, step_bias, rate_log, skip_gain, skip_proj, mixer_gain, proj_out)))
    wide_in = residual.astype(jnp.float32)
    segment, valid_mask = segments_of(doc_bounds, ROW_LEN)

    def forward(resid_in, *weights_in):

        def per_row(state_carry, row_data):
            row_in, row_seg, row_valid = row_data
            return (state_carry, jax.checkpoint(branch_row)(row_in, row_seg, row_valid, weights_in))
        final_carry, stacked = lax.scan(per_row, jnp.float32(0.0), (jnp.moveaxis(resid_in, 1, 0), segment, valid_mask))
        return jnp.moveaxis(stacked, 0, 1)
    branch, pullback = jax.vjp(forward, wide_in, *params)
    gradients = pullback(out_grad.astype(jnp.float32))
    output = (wide_in + branch).astype(jnp.bfloat16)
    grad_residual = out_grad.astype(jnp.float32) + gradients[0]
    return (output, grad_residual, gradients[1], gradients[2], gradients[3], gradients[4], gradients[5], gradients[6], gradients[7], gradients[8], gradients[9], gradients[10], gradients[11], gradients[12], gradients[13], gradients[14], gradients[15])
```

```python
import functools

import jax
import jax.numpy as jnp
from jax import lax
from jax.experimental import pallas as pl
from jax.experimental.pallas import tpu as pltpu
from jax.sharding import PartitionSpec as P

epsilon = 1e-05
BLOCK = 128
LANES = 128
LOG2E = 1.4426950408889634
f32 = jnp.float32
bf16 = jnp.bfloat16


def mm(a, b):
    return jnp.dot(a, b, preferred_element_type=f32)


def mm_nt(a, b):
    return lax.dot_general(a, b, (((1,), (1,)), ((), ())), preferred_element_type=f32)


def mm_tn(a, b):
    return lax.dot_general(a, b, (((0,), (0,)), ((), ())), preferred_element_type=f32)


def halves(w, axis):
    high = w.astype(bf16)
    low = (w - high.astype(f32)).astype(bf16)
    return jnp.concatenate([high, low], axis)


def iotas(rows, cols):
    return (
        lax.broadcasted_iota(jnp.int32, (rows, cols), 0),
        lax.broadcasted_iota(jnp.int32, (rows, cols), 1),
    )


def sigmoid(v):
    return 0.5 + 0.5 * jnp.tanh(0.5 * v)


def triangle(upper):
    row, col = iotas(BLOCK, BLOCK)
    keep = (col >= row) if upper else (col <= row)
    ones = jnp.where(keep, 1.0, 0.0).astype(bf16)
    return jnp.concatenate([ones, ones], 1)


def block_sums(values, heads, prefix_first):
    pair = halves(values, 0)
    below = mm(triangle(False), pair)
    above = mm(triangle(True), pair)
    lane = iotas(BLOCK, LANES)[1]
    first = lane < heads
    return jnp.where(first, below, above) if prefix_first else jnp.where(first, above, below)


def mask_lanes(meta, first_col, second_col, heads):
    lane = iotas(BLOCK, LANES)[1]
    return jnp.where(lane < heads, meta[:, first_col : first_col + 1], meta[:, second_col : second_col + 1])


def decay_parts(r2, sp, meta, heads):
    q2 = r2 - jnp.log(sp) * LOG2E
    lane = iotas(1, LANES)[1]
    end_row = jnp.where(lane < heads, r2[BLOCK - 1 : BLOCK, :], r2[0:1, :])
    reach = jnp.exp2(r2) * mask_lanes(meta, 6, 7, heads)
    weigh = jnp.exp2(end_row - q2) * mask_lanes(meta, 8, 9, heads)
    return q2, reach, weigh


def front_kernel(
    heads, width, blocks,
    res, halo, meta_ref, ng, wv, ws, wst, taps, step_bias, rate, ef2, eb2,
    normed_out, x_out, g_out, u_out, c_out, rs_out, sfl, sbl, coef, fin,
    ubuf, sf, stb, dfs, dbs,
):
    c = pl.program_id(0)
    inner = wv.shape[1]
    total = taps.shape[1]

    def normalize(values):
        wide = values.astype(f32)
        scale = lax.rsqrt(jnp.mean(wide * wide, -1, keepdims=True) + epsilon)
        return (wide * scale * ng[...]).astype(bf16)

    @pl.when(c == 0)
    def _():
        tail = normalize(halo[...])
        ubuf[0:8, 0:inner] = mm(tail, wv[...])[8:16]
        ubuf[0:8, inner:total] = mm(tail, ws[...])[8:16]
        sf[...] = jnp.zeros_like(sf)

    @pl.when(c > 0)
    def _():
        ubuf[0:8, :] = ubuf[BLOCK : BLOCK + 8, :]

    normed = normalize(res[...])
    normed_out[...] = normed
    ubuf[8 : BLOCK + 8, 0:inner] = mm(normed, wv[...])
    ubuf[8 : BLOCK + 8, inner:total] = mm(normed, ws[...])
    meta = meta_ref[...]

    pre = mm(normed, wst[...]) + step_bias[...]
    sp = jnp.maximum(pre, 0.0) + jnp.log1p(jnp.exp(-jnp.abs(pre)))
    r2 = block_sums(-sp * (rate[...] * LOG2E), heads, True)
    rs_out[:, 0:LANES] = r2
    rs_out[:, LANES : 2 * LANES] = sp
    _, reach, weigh = decay_parts(r2, sp, meta, heads)
    lane = iotas(1, LANES)[1]
    dvec = jnp.where(lane < heads, reach[BLOCK - 1 : BLOCK, :], reach[0:1, :])
    drow = halves(jnp.broadcast_to(dvec, (8, LANES)), 1)
    dfs[pl.ds(c, 1), :] = mm(drow, ef2[...])[0:1]
    dbs[pl.ds(c, 1), :] = mm(drow, eb2[...])[0:1]
    wpair = halves(weigh, 1)

    masks = [meta[:, j : j + 1] for j in range(3)]

    def convolve(cols):
        value = taps[4:5, cols] + taps[0:1, cols] * ubuf[8 : BLOCK + 8, cols]
        for j in range(1, 4):
            value = value + taps[j : j + 1, cols] * (ubuf[8 - j : BLOCK + 8 - j, cols] * masks[j - 1])
        u_out[:, cols] = ubuf[8 : BLOCK + 8, cols].astype(bf16)
        c_out[:, cols] = value.astype(bf16)
        return (value * sigmoid(value)).astype(bf16)

    state = convolve(slice(inner, total))
    g_out[...] = state
    state_t = jnp.transpose(state.astype(f32)).astype(bf16)
    n = (total - inner) // 4
    bf_t, bb_t = state_t[0:n], state_t[2 * n : 3 * n]
    dfrow, dbrow = dfs[pl.ds(c, 1), :], dbs[pl.ds(c, 1), :]
    for start in range(0, inner, 256):
        cols = slice(start, start + 256)
        x = convolve(cols)
        x_out[:, cols] = x
        wide = x.astype(f32)
        xwf = (wide * mm(wpair, ef2[:, cols])).astype(bf16)
        xwb = (wide * mm(wpair, eb2[:, cols])).astype(bf16)
        sfl[0, :, cols] = sf[:, cols].astype(bf16)
        sf[:, cols] = dfrow[:, cols] * sf[:, cols] + mm(bf_t, xwf)
        stb[c, :, cols] = mm(bb_t, xwb)

    @pl.when(c == blocks - 1)
    def _():
        fin[0:n, :] = sf[...]
        one = jnp.ones((1, inner), f32)

        def down(i, carry):
            k = blocks - 1 - i
            dfk, dbk = dfs[pl.ds(k, 1), :], dbs[pl.ds(k, 1), :]
            suffix_f, suffix_b = carry
            base = pl.multiple_of(k * 8, 8)
            coef[pl.ds(base + 1, 1), :] = suffix_f
            coef[pl.ds(base + 3, 1), :] = suffix_b
            coef[pl.ds(base + 4, 1), :] = dfk
            coef[pl.ds(base + 5, 1), :] = dbk
            carried = fin[n : 2 * n, :]
            sbl[k] = carried.astype(bf16)
            fin[n : 2 * n, :] = dbk * carried + stb[k]
            return suffix_f * dfk, suffix_b * dbk

        fin[n : 2 * n, :] = jnp.zeros((n, inner), f32)
        lax.fori_loop(0, blocks, down, (one, one))

        def up(k, carry):
            dfk, dbk = dfs[pl.ds(k, 1), :], dbs[pl.ds(k, 1), :]
            prefix_f, prefix_b = carry
            base = pl.multiple_of(k * 8, 8)
            coef[pl.ds(base, 1), :] = prefix_f
            coef[pl.ds(base + 2, 1), :] = prefix_b
            coef[pl.ds(base + 6, 1), :] = prefix_f * dfk
            coef[pl.ds(base + 7, 1), :] = prefix_b * dbk
            return prefix_f * dfk, prefix_b * dbk

        lax.fori_loop(0, blocks, up, (one, one))


def masked_scores(state, segrow, meta, n):
    bf, cf = state[:, 0:n], state[:, n : 2 * n]
    bb, cb = state[:, 2 * n : 3 * n], state[:, 3 * n : 4 * n]
    row, col = iotas(BLOCK, BLOCK)
    lower = row > col
    same = meta[:, 11:12] == segrow
    picked = jnp.where(lower, mm_nt(cf, bf), mm_nt(cb, bb))
    keep = jnp.where(row == col, 0.0, jnp.where(same, 1.0, 0.0))
    return bf, cf, bb, cb, lower, keep, picked * keep


def decay_matrix(h, heads, r2, q_t, lower):
    forward = r2[:, h : h + 1] - q_t[h : h + 1, :]
    k = heads + h
    reverse = r2[:, k : k + 1] - q_t[k : k + 1, :]
    return jnp.exp2(jnp.where(lower, forward, reverse))


def middle_kernel(
    heads, width, blocks,
    res, og_ref, normed_ref, x_ref, g_ref, rs_ref, meta_ref, segrow_ref, sfl, sbl, coef, entry_f, entry_b,
    wg, wo, skip, skip_gain, mixer_gain, ef2, eb2, eft, lanes,
    out, no_out, ggate_out, dy_out, direct_out, dtf, dtb, dfin, dmix, dskip_w, dskip_g,
    yv, dstf, drow, gpre,
):
    c = pl.program_id(0)
    inner = x_ref.shape[1]
    n = g_ref.shape[1] // 4

    @pl.when(c == 0)
    def _():
        dmix[...] = jnp.zeros_like(dmix)
        dskip_w[...] = jnp.zeros_like(dskip_w)
        dskip_g[...] = jnp.zeros_like(dskip_g)
        dfin[...] = jnp.zeros_like(dfin)

    meta = meta_ref[...]
    r2, sp = rs_ref[:, 0:LANES], rs_ref[:, LANES : 2 * LANES]
    q2, reach, _ = decay_parts(r2, sp, meta, heads)
    q_t = jnp.transpose(q2)
    bf, cf, bb, cb, lower, _, gm = masked_scores(g_ref[...], segrow_ref[0], meta, n)
    low_half, high_half = lanes[0:1, :], lanes[1:2, :]
    state_t = jnp.transpose(g_ref[...].astype(f32)).astype(bf16)
    cf_t, cb_t = state_t[n : 2 * n], state_t[3 * n : 4 * n]
    rpair = halves(reach, 1)
    valid = meta[:, 10:11]
    x_all = x_ref[...]
    skip_coef = mm(x_all, skip[...]) + skip_gain[...]
    spair = halves(skip_coef, 1)
    gpre[...] = mm(normed_ref[...], wg[...])

    square = jnp.zeros((BLOCK, 1), f32)
    per = LANES // width
    for p in range(inner // LANES):
        cols = slice(p * LANES, (p + 1) * LANES)
        x = x_ref[:, cols]
        mixes = [
            (decay_matrix(per * p + k, heads, r2, q_t, lower) * gm).astype(bf16) for k in range(per)
        ]
        spread = jnp.concatenate([x * low_half, x * high_half], 0)
        scanned = mm(jnp.concatenate(mixes, 1), spread)
        sf_in = (sfl[0, :, cols].astype(f32) + coef[0:1, cols] * entry_f[:, cols].astype(f32)).astype(bf16)
        sb_in = (sbl[0, :, cols].astype(f32) + coef[3:4, cols] * entry_b[:, cols].astype(f32)).astype(bf16)
        scanned = scanned + mm(rpair, ef2[:, cols]) * mm(cf, sf_in) + mm(rpair, eb2[:, cols]) * mm(cb, sb_in)
        mixed = scanned + mm(spair, ef2[:, cols]) * x.astype(f32)
        yv[:, cols] = mixed
        gate = gpre[:, cols]
        gated = mixed * (gate * sigmoid(gate)) * valid
        square = square + jnp.sum(gated * gated, -1, keepdims=True)
    scale = lax.rsqrt(square * (1.0 / inner) + epsilon)

    og = og_ref[...]
    gno = mm_nt(og, wo[...])
    cross = jnp.zeros((BLOCK, 1), f32)
    for start in range(0, inner, 256):
        cols = slice(start, start + 256)
        gate = gpre[:, cols]
        gated = yv[:, cols] * (gate * sigmoid(gate)) * valid
        weighted = gno[:, cols] * mixer_gain[:, cols]
        no_out[:, cols] = (gated * scale * mixer_gain[:, cols]).astype(bf16)
        cross = cross + jnp.sum(weighted * gated, -1, keepdims=True)
        dmix[0:1, cols] += jnp.sum(gno[:, cols] * (gated * scale), 0, keepdims=True)
    out[...] = (res[...].astype(f32) + mm(no_out[...], wo[...])).astype(bf16)
    cross = cross * (scale * scale * scale) * (1.0 / inner)

    dskip = jnp.zeros((BLOCK, LANES), f32)
    for start in range(0, inner, 256):
        cols = slice(start, start + 256)
        gate = gpre[:, cols]
        sig = sigmoid(gate)
        act = gate * sig
        mixed = yv[:, cols]
        gated = mixed * act * valid
        ggated = (scale * (gno[:, cols] * mixer_gain[:, cols]) - gated * cross) * valid
        gmixed = ggated * act
        ggate_out[:, cols] = (ggated * mixed * (sig * (1.0 + gate * (1.0 - sig)))).astype(bf16)
        dy_out[:, cols] = gmixed.astype(bf16)
        dskip = dskip + mm((gmixed * x_ref[:, cols].astype(f32)).astype(bf16), eft[cols, :])
    dskip_g[0:1, :] += jnp.sum(dskip, 0, keepdims=True)
    dskip_low = dskip.astype(bf16)
    dskip_w[...] += mm_tn(x_all, dskip_low)

    for start in range(0, inner, 256):
        cols = slice(start, start + 256)
        dy = dy_out[:, cols].astype(f32)
        direct = dy * mm(spair, ef2[:, cols]) + mm_nt(dskip_low, skip[cols, :])
        direct_out[:, cols] = direct.astype(bf16)
        dstf[c, :, cols] = mm(cf_t, (dy * mm(rpair, ef2[:, cols])).astype(bf16))
        step_b = mm(cb_t, (dy * mm(rpair, eb2[:, cols])).astype(bf16))
        carried = dfin[n : 2 * n, cols]
        dtb[0, :, cols] = carried.astype(bf16)
        dfin[n : 2 * n, cols] = coef[5:6, cols] * carried + step_b
    drow[pl.ds(c, 1), :] = coef[4:5, :]

    @pl.when(c == blocks - 1)
    def _():
        def down(i, carry):
            k = blocks - 1 - i
            carried = dfin[0:n, :]
            dtf[k] = carried.astype(bf16)
            dfin[0:n, :] = drow[pl.ds(k, 1), :] * carried + dstf[k]
            return carry

        lax.fori_loop(0, blocks, down, 0)


def scan_back_kernel(
    heads, width, blocks,
    x_ref, g_ref, rs_ref, meta_ref, segrow_ref, dy_ref, direct_ref, c_ref, sfl, sbl, coef, dtf, dtb,
    entry_f, entry_b, dentry_f, dentry_b, rate, ef2, eb2, eft, ebt, lanes,
    dca_out, dbias, dhead,
    del_fh, del_fl, del_bh, del_bl, kap_f, kap_b, dyr_f, dyr_b, xw_f, xw_b, s_f, s_b, t_f, t_b, ends,
):
    c = pl.program_id(0)
    inner = x_ref.shape[1]
    total = c_ref.shape[1]
    n = g_ref.shape[1] // 4

    @pl.when(c == 0)
    def _():
        dbias[...] = jnp.zeros_like(dbias)
        dhead[...] = jnp.zeros_like(dhead)

    meta = meta_ref[...]
    r2, sp = rs_ref[:, 0:LANES], rs_ref[:, LANES : 2 * LANES]
    q2, reach, weigh = decay_parts(r2, sp, meta, heads)
    q_t = jnp.transpose(q2)
    bf, cf, bb, cb, lower, keep, gm = masked_scores(g_ref[...], segrow_ref[0], meta, n)
    low_half, high_half = lanes[0:1, :], lanes[1:2, :]
    lower_low = jnp.where(lower, 1.0, 0.0).astype(bf16)
    rpair = halves(reach, 1)
    wpair = halves(weigh, 1)
    per = LANES // width
    dg = jnp.zeros((BLOCK, BLOCK), f32)
    for p in range(inner // LANES):
        cols = slice(p * LANES, (p + 1) * LANES)
        x, dy = x_ref[:, cols], dy_ref[:, cols]
        xf, dyf = x.astype(f32), dy.astype(f32)
        dy_spread = jnp.concatenate([dy * low_half, dy * high_half], 0)
        x_spread = jnp.concatenate([x * low_half, x * high_half], 0)
        dm = mm_nt(dy_spread, x)
        lows, ups = [], []
        for k in range(per):
            decay = decay_matrix(per * p + k, heads, r2, q_t, lower)
            dg = dg + dm[k * BLOCK : (k + 1) * BLOCK] * decay
            mix = (decay * gm).astype(bf16)
            mix_low = mix * lower_low
            lows.append(mix_low)
            ups.append(mix - mix_low)
        sf_in = (sfl[0, :, cols].astype(f32) + coef[0:1, cols] * entry_f[:, cols].astype(f32)).astype(bf16)
        sb_in = (sbl[0, :, cols].astype(f32) + coef[3:4, cols] * entry_b[:, cols].astype(f32)).astype(bf16)
        tf = (dtf[0, :, cols].astype(f32) + coef[1:2, cols] * dentry_f[:, cols].astype(f32)).astype(bf16)
        tb = (dtb[0, :, cols].astype(f32) + coef[2:3, cols] * dentry_b[:, cols].astype(f32)).astype(bf16)
        s_f[:, cols], s_b[:, cols], t_f[:, cols], t_b[:, cols] = sf_in, sb_in, tf, tb
        reach_f, reach_b = mm(rpair, ef2[:, cols]), mm(rpair, eb2[:, cols])
        weigh_f, weigh_b = mm(wpair, ef2[:, cols]), mm(wpair, eb2[:, cols])
        dyr_f[:, cols] = (dyf * reach_f).astype(bf16)
        dyr_b[:, cols] = (dyf * reach_b).astype(bf16)
        xwf, xwb = (xf * weigh_f).astype(bf16), (xf * weigh_b).astype(bf16)
        xw_f[:, cols], xw_b[:, cols] = xwf, xwb
        y_f = mm(jnp.concatenate(lows, 1), x_spread) + reach_f * mm(cf, sf_in)
        y_b = mm(jnp.concatenate(ups, 1), x_spread) + reach_b * mm(cb, sb_in)
        dw_f, dw_b = weigh_f * mm(bf, tf), weigh_b * mm(bb, tb)
        dx_f = mm_tn(jnp.concatenate(lows, 0), dy_spread) + dw_f
        dx_b = mm_tn(jnp.concatenate(ups, 0), dy_spread) + dw_b
        xdx_f, xdx_b = xf * dx_f, xf * dx_b
        kap_f[:, cols] = xdx_f.astype(bf16)
        kap_b[:, cols] = xdx_b.astype(bf16)
        for delta, high, rest in ((dyf * y_f - xdx_f, del_fh, del_fl), (dyf * y_b - xdx_b, del_bh, del_bl)):
            rounded = delta.astype(bf16)
            high[:, cols] = rounded
            rest[:, cols] = (delta - rounded.astype(f32)).astype(bf16)
        through_f = coef[4:5, cols] * jnp.sum(tf.astype(f32) * sf_in.astype(f32), 0, keepdims=True)
        through_b = coef[5:6, cols] * jnp.sum(tb.astype(f32) * sb_in.astype(f32), 0, keepdims=True)
        ends[0:1, cols] = through_f + jnp.sum(xf * dw_f, 0, keepdims=True)
        ends[1:2, cols] = through_b + jnp.sum(xf * dw_b, 0, keepdims=True)
        pre = c_ref[:, cols].astype(f32)
        sig = sigmoid(pre)
        dc = (dx_f + dx_b + direct_ref[:, cols].astype(f32)) * (sig * (1.0 + pre * (1.0 - sig)))
        dca_out[:, cols] = dc.astype(bf16)
        dbias[0:1, cols] += jnp.sum(dc, 0, keepdims=True)

    dg = dg * keep
    dg_low = jnp.where(lower, dg, 0.0)
    dg_f = dg_low.astype(bf16)
    dg_b = (dg - dg_low).astype(bf16)
    d_bf = mm_tn(dg_f, cf) + mm_nt(xw_f[...], t_f[...])
    d_cf = mm(dg_f, bf) + mm_nt(dyr_f[...], s_f[...])
    d_bb = mm_tn(dg_b, cb) + mm_nt(xw_b[...], t_b[...])
    d_cb = mm(dg_b, bb) + mm_nt(dyr_b[...], s_b[...])
    d_state = jnp.concatenate([d_bf, d_cf, d_bb, d_cb], 1)
    tail = slice(inner, total)
    pre = c_ref[:, tail].astype(f32)
    sig = sigmoid(pre)
    dc = d_state * (sig * (1.0 + pre * (1.0 - sig)))
    dca_out[:, tail] = dc.astype(bf16)
    dbias[0:1, tail] += jnp.sum(dc, 0, keepdims=True)

    delta = mm(del_fh[...], eft[...]) + mm(del_bh[...], ebt[...]) + mm(del_fl[...], eft[...]) + mm(del_bl[...], ebt[...])
    kap = mm(kap_f[...], eft[...]) + mm(kap_b[...], ebt[...])
    end_pair = halves(jnp.broadcast_to(ends[0:1, :], (8, inner)), 0)
    end_f = mm(end_pair, eft[...])
    end_pair = halves(jnp.broadcast_to(ends[1:2, :], (8, inner)), 0)
    end_b = mm(end_pair, ebt[...])
    end = end_f[0:1] + end_f[8:9] + end_b[0:1] + end_b[8:9]
    dld = block_sums(delta, heads, False) + end
    phi = jnp.where(sp < 1e-3, 1.0 - 0.5 * sp, (1.0 - jnp.exp(-sp)) / jnp.maximum(sp, 1e-3))
    pull = dld * rate[...]
    dstep = kap * phi - pull * (phi * sp)
    dca_out[:, total : total + LANES] = dstep.astype(bf16)
    dhead[0:1, :] += jnp.sum(dstep, 0, keepdims=True)
    dhead[1:2, :] += jnp.sum(-pull * sp, 0, keepdims=True)


def conv_back_kernel(blocks, dca, nxt, halo, u, meta_ref, taps, dall, dtaps, buf):
    c = pl.program_id(0)
    total = u.shape[1]

    @pl.when(c == 0)
    def _():
        dtaps[...] = jnp.zeros_like(dtaps)

    masks = [meta_ref[:, 3 + j : 4 + j] for j in range(3)]
    for start in range(0, total, 256):
        cols = slice(start, start + 256)
        dc = dca[:, cols].astype(f32)
        buf[0:BLOCK, cols] = dc
        buf[BLOCK : BLOCK + 16, cols] = jnp.where(
            c == blocks - 1, halo[:, cols].astype(f32), nxt[:, cols].astype(f32)
        )
        uv = u[:, cols].astype(f32)
        grad = taps[0:1, cols] * dc
        dtaps[0:1, cols] += jnp.sum(uv * dc, 0, keepdims=True)
        for j in range(1, 4):
            moved = buf[j : BLOCK + j, cols] * masks[j - 1]
            grad = grad + taps[j : j + 1, cols] * moved
            dtaps[j : j + 1, cols] += jnp.sum(uv * moved, 0, keepdims=True)
        dall[:, cols] = grad.astype(bf16)
    dall[:, total:] = dca[:, total:]


def tail_kernel(res, og, ggate, dall, ng, wg, wrest, out, dng):
    c = pl.program_id(0)

    @pl.when(c == 0)
    def _():
        dng[...] = jnp.zeros_like(dng)

    grad = mm_nt(ggate[...], wg[...]) + mm_nt(dall[...], wrest[...])
    wide = res[...].astype(f32)
    scale = lax.rsqrt(jnp.mean(wide * wide, -1, keepdims=True) + epsilon)
    gained = grad * ng[...]
    cube = scale * scale * scale * jnp.mean(gained * wide, -1, keepdims=True)
    out[...] = og[...].astype(f32) + scale * gained - wide * cube
    dng[0:1, :] += jnp.sum(grad * (wide * scale), 0, keepdims=True)


def row_spec(rows, cols):
    return pl.BlockSpec((rows, cols), lambda c: (c, 0))


def plane_spec(rows, cols):
    return pl.BlockSpec((1, rows, cols), lambda c: (c, 0, 0))


def whole_spec(array):
    rank = len(array.shape)
    return pl.BlockSpec(tuple(array.shape), lambda c: (0,) * rank, pipeline_mode=pl.Buffered(1))


def shaped(shape, kind):
    return jax.ShapeDtypeStruct(shape, kind)


def shards(
    residual,
    out_grad,
    doc_bounds,
    norm_gain,
    proj_gate,
    proj_value,
    proj_state,
    proj_step,
    conv_value,
    conv_value_bias,
    conv_state,
    conv_state_bias,
    step_bias,
    rate_log,
    skip_gain,
    skip_proj,
    mixer_gain,
    proj_out,
):
    length, row_count, model_width = residual.shape
    assert row_count == 1 and length % BLOCK == 0
    parts = lax.axis_size("mp")
    me = lax.axis_index("mp")
    own_heads = rate_log.shape[0]
    own_chan = proj_value.shape[1]
    heads = own_heads * parts
    inner = own_chan * parts
    width = own_chan // own_heads
    state_all = proj_state.shape[1]
    n = state_all // 4
    total = inner + state_all
    blocks = length // BLOCK
    full_len = length * parts
    res = residual[:, 0, :]
    og = out_grad[:, 0, :]

    def gather(values, axis):
        return lax.all_gather(values, "mp", axis=axis, tiled=True)

    right = [(i, i + 1) for i in range(parts - 1)]
    left = [(i + 1, i) for i in range(parts - 1)]

    halo = lax.ppermute(res[length - 16 :], "mp", right)
    wv = gather(proj_value, 1)
    small = jnp.concatenate(
        [conv_value.reshape(-1), conv_value_bias, mixer_gain, step_bias, rate_log, skip_gain]
    )
    small = gather(small[None], 0)
    sizes = [4 * own_chan, own_chan, own_chan, 2 * own_heads, own_heads, own_heads]
    at, pieces = 0, []
    for size in sizes:
        pieces.append(small[:, at : at + size])
        at += size
    conv_v = jnp.moveaxis(pieces[0].reshape(parts, 4, own_chan), 0, 1).reshape(4, inner)
    bias_v, gain_m = pieces[1].reshape(1, inner), pieces[2].reshape(1, inner)

    def by_direction(values):
        lead = values.shape[:-1]
        return jnp.swapaxes(values.reshape(lead + (heads, 2)), -1, -2).reshape(lead + (2 * heads,))

    def pad_lanes(values):
        return jnp.pad(values, [(0, 0)] * (values.ndim - 1) + [(0, LANES - values.shape[-1])])

    bias_s = pad_lanes(by_direction(pieces[3].reshape(1, 2 * heads)))
    rate = pad_lanes(jnp.tile(jnp.exp(pieces[4].reshape(1, heads)), (1, 2)))
    gain_s = pad_lanes(pieces[5].reshape(1, heads))
    wst = pad_lanes(by_direction(gather(proj_step, 1)))
    skip = pad_lanes(gather(skip_proj, 0))
    wg = gather(proj_gate, 1)
    wo = gather(proj_out, 0)
    taps = jnp.concatenate(
        [
            jnp.concatenate([conv_v, conv_state], 1),
            jnp.concatenate([bias_v, conv_state_bias[None]], 1),
            jnp.zeros((3, total), f32),
        ],
        0,
    )
    ng = norm_gain[None]

    bounds = doc_bounds[0]

    def segment_at(places):
        found = jnp.sum((places[:, None] >= bounds[None, :]).astype(jnp.int32), -1)
        return jnp.where(places < 0, -1, jnp.where(places >= full_len, -2, found))

    pos = me * length + jnp.arange(length, dtype=jnp.int32)
    base = pos - pos % BLOCK
    seg = segment_at(pos)
    columns = [segment_at(pos - j) == seg for j in (1, 2, 3)]
    columns += [segment_at(pos + j) == seg for j in (1, 2, 3)]
    columns += [segment_at(base - 1) == seg, segment_at(base + BLOCK) == seg]
    columns += [segment_at(base + BLOCK - 1) == seg, segment_at(base) == seg]
    columns += [pos < bounds[-1]]
    meta = jnp.stack([v.astype(f32) for v in columns] + [seg.astype(f32)], 1)
    meta = pad_lanes(meta)
    segrow = seg.astype(f32).reshape(blocks, 1, BLOCK)

    chan_head = jnp.arange(inner) // width
    lane_id = jnp.arange(LANES)
    spread_f = (lane_id[:, None] == chan_head[None, :]).astype(bf16)
    spread_b = (lane_id[:, None] == chan_head[None, :] + heads).astype(bf16)
    ef2, eb2 = jnp.concatenate([spread_f] * 2, 0), jnp.concatenate([spread_b] * 2, 0)
    eft, ebt = spread_f.T, spread_b.T
    half = (jnp.arange(LANES) < width).astype(bf16)
    lanes = jnp.concatenate([half[None], 1 - half[None], jnp.zeros((14, LANES), bf16)], 0)

    params = pltpu.CompilerParams(dimension_semantics=("arbitrary",), vmem_limit_bytes=60 * 1024 * 1024)

    front_in = (res, halo, meta, ng, wv, proj_state, wst, taps, bias_s, rate, ef2, eb2)
    normed, x, g, u, cpre, rs, sfl, sbl, coef, fin = pl.pallas_call(
        functools.partial(front_kernel, heads, width, blocks),
        grid=(blocks,),
        in_specs=[row_spec(BLOCK, model_width), whole_spec(halo), row_spec(BLOCK, LANES)]
        + [whole_spec(v) for v in front_in[3:]],
        out_specs=[
            row_spec(BLOCK, model_width),
            row_spec(BLOCK, inner),
            row_spec(BLOCK, state_all),
            row_spec(BLOCK, total),
            row_spec(BLOCK, total),
            row_spec(BLOCK, 2 * LANES),
            plane_spec(n, inner),
            pl.BlockSpec((blocks, n, inner), lambda c: (0, 0, 0)),
            pl.BlockSpec((blocks * 8, inner), lambda c: (0, 0)),
            pl.BlockSpec((2 * n, inner), lambda c: (0, 0)),
        ],
        out_shape=[
            shaped((length, model_width), bf16),
            shaped((length, inner), bf16),
            shaped((length, state_all), bf16),
            shaped((length, total), bf16),
            shaped((length, total), bf16),
            shaped((length, 2 * LANES), f32),
            shaped((blocks, n, inner), bf16),
            shaped((blocks, n, inner), bf16),
            shaped((blocks * 8, inner), f32),
            shaped((2 * n, inner), f32),
        ],
        scratch_shapes=[
            pltpu.VMEM((BLOCK + 8, total), f32),
            pltpu.VMEM((n, inner), f32),
            pltpu.VMEM((blocks, n, inner), f32),
            pltpu.VMEM((blocks, inner), f32),
            pltpu.VMEM((blocks, inner), f32),
        ],
        compiler_params=params,
        name="front",
    )(*front_in)

    decay_f, decay_b = coef[blocks * 8 - 2 : blocks * 8 - 1], coef[blocks * 8 - 1 :]

    def chain(first, factor, pairs):
        got = lax.ppermute(first.astype(bf16), "mp", pairs)
        for _ in range(parts - 2):
            got = lax.ppermute((first + factor * got.astype(f32)).astype(bf16), "mp", pairs)
        return got

    entry_f = chain(fin[:n], decay_f, right)
    entry_b = chain(fin[n:], decay_b, left)

    middle_in = (
        res, og, normed, x, g, rs, meta, segrow, sfl, sbl, coef, entry_f, entry_b,
        wg, wo, skip, gain_s, gain_m, ef2, eb2, eft, lanes,
    )
    coef_spec = pl.BlockSpec((8, inner), lambda c: (c, 0))
    out, normed_out, ggate, dy, direct, dtf, dtb, dfin, dmix, dskip_w, dskip_g = pl.pallas_call(
        functools.partial(middle_kernel, heads, width, blocks),
        grid=(blocks,),
        in_specs=[
            row_spec(BLOCK, model_width),
            row_spec(BLOCK, model_width),
            row_spec(BLOCK, model_width),
            row_spec(BLOCK, inner),
            row_spec(BLOCK, state_all),
            row_spec(BLOCK, 2 * LANES),
            row_spec(BLOCK, LANES),
            plane_spec(1, BLOCK),
            plane_spec(n, inner),
            plane_spec(n, inner),
            coef_spec,
        ]
        + [whole_spec(v) for v in middle_in[11:]],
        out_specs=[
            row_spec(BLOCK, model_width),
            row_spec(BLOCK, inner),
            row_spec(BLOCK, inner),
            row_spec(BLOCK, inner),
            row_spec(BLOCK, inner),
            pl.BlockSpec((blocks, n, inner), lambda c: (0, 0, 0)),
            plane_spec(n, inner),
            pl.BlockSpec((2 * n, inner), lambda c: (0, 0)),
            pl.BlockSpec((8, inner), lambda c: (0, 0)),
            pl.BlockSpec((inner, LANES), lambda c: (0, 0)),
            pl.BlockSpec((8, LANES), lambda c: (0, 0)),
        ],
        out_shape=[
            shaped((length, model_width), bf16),
            shaped((length, inner), bf16),
            shaped((length, inner), bf16),
            shaped((length, inner), bf16),
            shaped((length, inner), bf16),
            shaped((blocks, n, inner), bf16),
            shaped((blocks, n, inner), bf16),
            shaped((2 * n, inner), f32),
            shaped((8, inner), f32),
            shaped((inner, LANES), f32),
            shaped((8, LANES), f32),
        ],
        scratch_shapes=[
            pltpu.VMEM((BLOCK, inner), f32),
            pltpu.VMEM((blocks, n, inner), f32),
            pltpu.VMEM((blocks, inner), f32),
            pltpu.VMEM((BLOCK, inner), f32),
        ],
        compiler_params=params,
        name="middle",
    )(*middle_in)

    dentry_f = chain(dfin[:n], decay_f, left)
    dentry_b = chain(dfin[n:], decay_b, right)

    def outer_sum(left_op, right_op):
        return lax.dot_general(left_op, right_op, (((0,), (0,)), ((), ())), preferred_element_type=f32)

    def reduce_rows(values, axis):
        mine = lax.psum_scatter(values.astype(bf16), "mp", scatter_dimension=axis, tiled=True)
        return lax.psum(mine, "dp").astype(f32)

    grad_proj_out = reduce_rows(outer_sum(normed_out, og), 0)
    grad_proj_gate = reduce_rows(outer_sum(normed, ggate), 1)

    back_in = (
        x, g, rs, meta, segrow, dy, direct, cpre, sfl, sbl, coef, dtf, dtb,
        entry_f, entry_b, dentry_f, dentry_b, rate, ef2, eb2, eft, ebt, lanes,
    )
    wide_total = total + LANES
    dca, dbias, dhead = pl.pallas_call(
        functools.partial(scan_back_kernel, heads, width, blocks),
        grid=(blocks,),
        in_specs=[
            row_spec(BLOCK, inner),
            row_spec(BLOCK, state_all),
            row_spec(BLOCK, 2 * LANES),
            row_spec(BLOCK, LANES),
            plane_spec(1, BLOCK),
            row_spec(BLOCK, inner),
            row_spec(BLOCK, inner),
            row_spec(BLOCK, total),
            plane_spec(n, inner),
            plane_spec(n, inner),
            coef_spec,
            plane_spec(n, inner),
            plane_spec(n, inner),
        ]
        + [whole_spec(v) for v in back_in[13:]],
        out_specs=[
            row_spec(BLOCK, wide_total),
            pl.BlockSpec((8, total), lambda c: (0, 0)),
            pl.BlockSpec((8, LANES), lambda c: (0, 0)),
        ],
        out_shape=[
            shaped((length, wide_total), bf16),
            shaped((8, total), f32),
            shaped((8, LANES), f32),
        ],
        scratch_shapes=[pltpu.VMEM((BLOCK, inner), bf16)] * 10
        + [pltpu.VMEM((n, inner), bf16)] * 4
        + [pltpu.VMEM((8, inner), f32)],
        compiler_params=params,
        name="scan_back",
    )(*back_in)

    halo_back = lax.ppermute(dca[:16], "mp", left)
    dall, dtaps = pl.pallas_call(
        functools.partial(conv_back_kernel, blocks),
        grid=(blocks,),
        in_specs=[
            row_spec(BLOCK, wide_total),
            pl.BlockSpec((16, wide_total), lambda c: (jnp.minimum((c + 1) * (BLOCK // 16), length // 16 - 1), 0)),
            whole_spec(halo_back),
            row_spec(BLOCK, total),
            row_spec(BLOCK, LANES),
            whole_spec(taps),
        ],
        out_specs=[row_spec(BLOCK, wide_total), pl.BlockSpec((8, total), lambda c: (0, 0))],
        out_shape=[shaped((length, wide_total), bf16), shaped((8, total), f32)],
        scratch_shapes=[pltpu.VMEM((BLOCK + 16, total), f32)],
        compiler_params=params,
        name="conv_back",
    )(dca, dca, halo_back, u, meta, taps)

    grads_late = outer_sum(normed, dall)
    grad_step = jnp.swapaxes(
        grads_late[:, total : total + 2 * heads].reshape(model_width, 2, heads), 1, 2
    ).reshape(model_width, 2 * heads)
    late = [grads_late[:, :inner], grads_late[:, inner:total], grad_step]
    late = jnp.concatenate(
        [v.reshape(model_width, parts, v.shape[1] // parts) for v in late], 2
    ).reshape(model_width, -1)
    late_own = reduce_rows(late, 1)
    grad_proj_value = late_own[:, :own_chan]
    own_state = state_all // parts
    grad_proj_state = gather(late_own[:, own_chan : own_chan + own_state].astype(bf16), 1).astype(f32)
    grad_proj_step = late_own[:, own_chan + own_state :]

    wrest = jnp.concatenate([wv, proj_state, wst], 1)
    tail_in = (res, og, ggate, dall, ng, wg, wrest)
    grad_residual, dng = pl.pallas_call(
        tail_kernel,
        grid=(blocks,),
        in_specs=[
            row_spec(BLOCK, model_width),
            row_spec(BLOCK, model_width),
            row_spec(BLOCK, inner),
            row_spec(BLOCK, wide_total),
        ]
        + [whole_spec(v) for v in tail_in[4:]],
        out_specs=[row_spec(BLOCK, model_width), pl.BlockSpec((8, model_width), lambda c: (0, 0))],
        out_shape=[shaped((length, model_width), f32), shaped((8, model_width), f32)],
        compiler_params=params,
        name="tail",
    )(*tail_in)

    small_grads = [
        dng[0],
        dtaps[:4, inner:].reshape(-1),
        dbias[0, inner:],
        dtaps[:4, :inner].reshape(-1),
        dbias[0, :inner],
        dmix[0],
        dskip_w[:, :heads].reshape(-1),
        dhead[0, : 2 * heads].reshape(2, heads).T.reshape(-1),
        dhead[1, :heads] + dhead[1, heads : 2 * heads],
        dskip_g[0, :heads],
    ]
    flat = lax.psum(jnp.concatenate(small_grads), ("dp", "mp"))
    at, sums = 0, []
    for v in small_grads:
        sums.append(flat[at : at + v.shape[0]])
        at += v.shape[0]

    def own(values, axis):
        size = values.shape[axis] // parts
        return lax.dynamic_slice_in_dim(values, me * size, size, axis)

    return (
        out[:, None, :],
        grad_residual[:, None, :],
        sums[0],
        grad_proj_gate,
        grad_proj_value,
        grad_proj_state,
        grad_proj_step,
        own(sums[3].reshape(4, inner), 1),
        own(sums[4], 0),
        sums[1].reshape(4, state_all),
        sums[2],
        own(sums[7], 0),
        own(sums[8], 0),
        own(sums[9], 0),
        own(sums[6].reshape(inner, heads), 0),
        own(sums[5], 0),
        grad_proj_out,
    )


def solution(mesh):
    return jax.shard_map(
        shards,
        mesh=mesh,
        in_specs=(
            P("mp", "dp", None),
            P("mp", "dp", None),
            P("dp", None),
            P(),
            P(None, "mp"),
            P(None, "mp"),
            P(),
            P(None, "mp"),
            P(None, "mp"),
            P("mp"),
            P(),
            P(),
            P("mp"),
            P("mp"),
            P("mp"),
            P("mp", None),
            P("mp"),
            P("mp", None),
        ),
        out_specs=(
            P("mp", "dp", None),
            P("mp", "dp", None),
            P(),
            P(None, "mp"),
            P(None, "mp"),
            P(),
            P(None, "mp"),
            P(None, "mp"),
            P("mp"),
            P(),
            P(),
            P("mp"),
            P("mp"),
            P("mp"),
            P("mp", None),
            P("mp"),
            P("mp", None),
        ),
        check_vma=False,
    )
```
